128 devices in a mesh: date: 8 (over y, z_lo), space: 16 (over x, z_hi, core).
Axes of the slice: x: 4, y: 4, z: 4 (z_hi: 2, z_lo: 2; z = z_hi * 2 + z_lo), core: 2. Of those that a mesh axis runs over, the one named last changes fastest.
Arguments:
- acquisitions: bfloat16 [2, 128, 384, 2304], P(None, 'date', 'space'), may hold values from -6 to 6
- valid_dates: int32 [128, 384, 2304], P('date', 'space'), may hold values 0 or 1
Outputs:
- linked: float32 [2, 128, 64, 768], P(None, 'date', 'space')
The draws below stay inside these ranges and needn't reach their ends.
All inputs are finite; a program needn't handle non-finite values. No bound on the sum of `valid_dates` on one device may be relied on, other than what follows from the above.
Results may differ from the reference program's by a relative error of at most 0.0028.
Values may be sent and summed in bfloat16 or wider, within the bound.
A program may use at most 256 MiB of HBM per device.

```python
import jax
import jax.numpy as jnp
from jax import lax

DATES = 128
BOX_ROWS = 15
BOX_COLS = 7
STEP_ROWS = 3
STEP_COLS = 6
ITERS = 4
MARGIN = 6
NBOX = 105
ROWS = 2304
COLS = 384
OUTROWS = 768


def set_ends(drawn, key, low, high):
    longest = drawn.shape.index(max(drawn.shape))
    spots = []
    for shift in (0, 1):
        where = [jax.random.randint(jax.random.fold_in(key, axis), (), 0, length) for axis, length in enumerate(drawn.shape)]
        where[longest] = (where[longest] + shift) % drawn.shape[longest]
        spots.append(tuple(where))
    return drawn.at[spots[0]].set(low).at[spots[1]].set(high)


def levels(stream_key, dims, shards, smallest, largest):
    factor_of = 1.0
    for position, shards_of in shards:
        steps = jax.random.uniform(jax.random.fold_in(jax.random.fold_in(stream_key, 6), position), (shards_of,), jnp.float32, smallest / len(shards), largest / len(shards))
        factor_of = factor_of * jnp.repeat(jnp.exp(steps), dims[position] // shards_of).reshape((-1,) + (1,) * (len(dims) - 1 - position))
    return factor_of


def centred(stream_key, shape, spread, bound, split=(), kind=jnp.bfloat16):
    values = jax.random.normal(stream_key, shape, jnp.float32) * spread
    if len(split) > 0:
        values = levels(stream_key, shape, split, -0.22, 0.18) * values
    return jnp.clip(values, min=-bound, max=bound).astype(kind)


def setup_inputs(seed: int = 0) -> dict:
    key_list = jax.random.split(jax.random.key(seed), 3)
    return {
        "acquisitions": centred(key_list[0], (2, DATES, COLS, ROWS), 1.0, 6.0, ((1, 8), (2, 16))),
        "valid_dates": set_ends((jax.random.randint(key_list[1], (DATES, COLS, ROWS), 0, 4) < 3).astype(jnp.int32), jax.random.fold_in(key_list[1], 1), 0, 1),
    }


POWER_EPS = 1e-05

def reference(acquisitions, valid_dates):
    masked = acquisitions * valid_dates.astype(jnp.bfloat16)[None]
    masked = jnp.swapaxes(masked, 2, 3)
    left_pad = STEP_COLS // 2
    framed = jnp.pad(masked, ((0, 0), (0, 0), (MARGIN, MARGIN), (left_pad, BOX_COLS - STEP_COLS)))
    out_cols = COLS // STEP_COLS
    span = STEP_COLS * (out_cols - 1) + 1

    def link_row(out_row):
        band_rows = lax.dynamic_slice_in_dim(framed, out_row * STEP_ROWS, BOX_ROWS, 2)
        window = jnp.stack([band_rows[..., k:k + span:STEP_COLS] for k in range(BOX_COLS)], axis=3)
        window = window.astype(jnp.float32)
        real_sum = jnp.einsum('adrkc,aerkc->cde', window, window, precision=lax.Precision.HIGHEST)
        cross_sum = jnp.einsum('drkc,erkc->cde', window[1], window[0], precision=lax.Precision.HIGHEST)
        energy = jnp.diagonal(real_sum, axis1=1, axis2=2) / NBOX + POWER_EPS
        factor = lax.rsqrt(energy)
        weights = factor[:, :, None] * factor[:, None, :] / NBOX
        coh_real = (real_sum * weights).astype(jnp.bfloat16).astype(jnp.float32)
        coh_imag = ((cross_sum - jnp.swapaxes(cross_sum, 1, 2)) * weights).astype(jnp.bfloat16).astype(jnp.float32)
        vec_real = jnp.ones((out_cols, DATES), jnp.float32)
        vec_imag = jnp.zeros((out_cols, DATES), jnp.float32)
        for sweep in range(ITERS):
            real_out = jnp.einsum('cde,ce->cd', coh_real, vec_real, precision=lax.Precision.HIGHEST) - jnp.einsum('cde,ce->cd', coh_imag, vec_imag, precision=lax.Precision.HIGHEST)
            imag_out = jnp.einsum('cde,ce->cd', coh_imag, vec_real, precision=lax.Precision.HIGHEST) + jnp.einsum('cde,ce->cd', coh_real, vec_imag, precision=lax.Precision.HIGHEST)
            total = lax.optimization_barrier(jnp.sum(real_out * real_out + imag_out * imag_out, axis=1)) / DATES + POWER_EPS
            norm_factor = lax.rsqrt(total)[:, None]
            vec_real = real_out * norm_factor
            vec_imag = imag_out * norm_factor
            if sweep + 1 < ITERS:
                vec_real = vec_real.astype(jnp.bfloat16).astype(jnp.float32)
                vec_imag = vec_imag.astype(jnp.bfloat16).astype(jnp.float32)
        return jnp.stack([vec_real, vec_imag])
    rows_out = lax.map(link_row, jnp.arange(OUTROWS, dtype=jnp.int32))
    return jnp.transpose(rows_out, (1, 3, 2, 0))
```

```python
import jax
import jax.numpy as jnp
from jax import lax
from jax.experimental import pallas as pl
from jax.experimental.pallas import tpu as pltpu
from jax.sharding import PartitionSpec as P

MESH = pl.DeviceIdType.MESH
EPS = 1e-05
NBOX = 105
NDATE = 8
NSPACE = 16
LD = 16
LC = 24
ROWS = 2304
WIN = 96
WIDE = 256
TAIL = 44
TILES = ROWS // 128 + 2

CHUNKS = (
    (4, 9, (0, 4), 4, ((8, 0, 5),)),
    (9, 16, (4, 10), 9, ((15, 5, 5),)),
    (16, 24, (10, 16), 16, ((22, 10, 5), (23, 15, 5))),
    (24, 31, (16, 22), 24, ((30, 20, 2),)),
)
BLOCKS = 31


def block_of(col):
    if col < 0:
        return col + 3
    for first, _, (low, high), start, _ in CHUNKS:
        if low <= col < high:
            return start + col - low


def tails_of(out_col):
    low, high = 6 * out_col - 3, 6 * out_col + 3
    found = []
    for block, first, count in [(3, -3, 3)] + [t for ch in CHUNKS for t in ch[4]]:
        start, stop = max(low, first), min(high, first + count - 1)
        if start <= stop:
            found.append((block, start - first, stop - first))
    return found


def dot(left, right):
    return lax.dot_general(
        left, right, (((1,), (0,)), ((), ())), preferred_element_type=jnp.float32
    )


def dot_t(left, right):
    return lax.dot_general(
        left, right, (((1,), (1,)), ((), ())), preferred_element_type=jnp.float32
    )


def split(value):
    high = value.astype(jnp.bfloat16)
    low = (value - high.astype(jnp.float32)).astype(jnp.bfloat16)
    return high, low


def kernel(
    acq_hbm, val_hbm, out_ref,
    acq, val, masked, send, recv, squares, band, back, home,
    in_sem, send_sem, recv_sem, side_send, side_recv, own_sem,
    back_send, back_recv, back_own,
):
    me = lax.axis_index("date")
    strip = lax.axis_index("space")
    right = lax.rem(strip + 1, NSPACE)
    left = lax.rem(strip + NSPACE - 1, NSPACE)
    my_rows = pl.ds(pl.multiple_of(me * LD, LD), LD)

    def load(octet):
        cols = pl.ds(8 * octet, 8)
        return (
            pltpu.make_async_copy(
                acq_hbm.at[:, :, cols, :], acq.at[:, :, cols, :], in_sem.at[0, octet]
            ),
            pltpu.make_async_copy(
                val_hbm.at[:, cols, :], val.at[:, cols, :], in_sem.at[1, octet]
            ),
        )

    for octet in (2, 0, 1):
        for copy in load(octet):
            copy.start()

    barrier = pltpu.get_barrier_semaphore()
    for hop in range(1, NDATE):
        pl.semaphore_signal(
            barrier, inc=1, device_id=(lax.rem(me + hop, NDATE), strip), device_id_type=MESH
        )
    for hop in range(NDATE):
        pl.semaphore_signal(
            barrier, inc=1, device_id=(lax.rem(me + hop, NDATE), left), device_id_type=MESH
        )

    row = lax.broadcasted_iota(jnp.int32, (2 * WIN, WIDE), 0)
    lane = lax.broadcasted_iota(jnp.int32, (2 * WIN, WIDE), 1)
    row = jnp.where(row >= WIN, row - WIN, row)
    band[...] = jnp.where((lane >= 3 * row) & (lane <= 3 * row + 14), 1.0, 0.0)

    masked[0] = jnp.zeros((2 * LD * LC, 128), jnp.float32)
    masked[TILES - 1] = jnp.zeros((2 * LD * LC, 128), jnp.float32)

    def mask(octet):
        for copy in load(octet):
            copy.wait()

        def body(date, carry):
            cols = pl.ds(8 * octet, 8)
            valid = val[date, cols, :].astype(jnp.float32)
            for part in range(2):
                value = acq[part, date, cols, :].astype(jnp.float32) * valid
                at = pl.multiple_of(part * (LD * LC) + date * LC + 8 * octet, 8)
                for tile in range(TILES - 2):
                    masked[1 + tile, pl.ds(at, 8), :] = value[:, tile * 128 : tile * 128 + 128]
            return carry

        lax.fori_loop(0, LD, body, 0)

    def strip_tiles(part, col, tile, count):
        at = pl.ds(part * (LD * LC) + col, LD, stride=LC)
        return jnp.concatenate([masked[tile + j, at, :] for j in range(count)], axis=1)

    def pack_main(low, high, start):
        def body(step, carry):
            col = low + step // 2
            part = step % 2
            block = start + step // 2
            for k in range(NDATE):
                at = 122 + 288 * k
                tile, shift = at // 128, at % 128
                value = strip_tiles(part, col, tile, 3)
                send[k, block, part] = value[:, shift : shift + WIDE].astype(jnp.bfloat16)
            return carry

        lax.fori_loop(0, 2 * (high - low), body, 0)

    def pack_tail(block, first, count):
        place = lax.broadcasted_iota(jnp.int32, (LD, WIDE), 1)

        def body(part, carry):
            for k in range(NDATE):
                at = 122 + 288 * k + WIDE
                tile, shift = at // 128, at % 128
                total = jnp.zeros((LD, WIDE), jnp.float32)
                for q in range(count):
                    value = strip_tiles(part, first + q, tile, 2)
                    moved = pltpu.roll(value, (TAIL * q - shift) % WIDE, 1)
                    here = (place >= TAIL * q) & (place < TAIL * (q + 1))
                    total = jnp.where(here, moved, total)
                send[k, block, part] = total.astype(jnp.bfloat16)
            return carry

        lax.fori_loop(0, 2, body, 0)

    def own_copy(chunk, hop):
        low, high = CHUNKS[chunk][:2]
        to = lax.rem(me + hop, NDATE)
        return pltpu.make_async_remote_copy(
            src_ref=send.at[to, low:high],
            dst_ref=recv.at[low:high, :, my_rows],
            send_sem=send_sem.at[chunk, hop],
            recv_sem=recv_sem.at[chunk, hop],
            device_id=(to, strip),
            device_id_type=MESH,
        )

    def own_local(chunk):
        low, high = CHUNKS[chunk][:2]
        return pltpu.make_async_copy(
            send.at[me, low:high], recv.at[low:high, :, my_rows], own_sem.at[chunk]
        )

    def side_copy(hop):
        to = lax.rem(me + hop, NDATE)
        return pltpu.make_async_remote_copy(
            src_ref=send.at[to, 0:4],
            dst_ref=recv.at[0:4, :, my_rows],
            send_sem=side_send.at[hop],
            recv_sem=side_recv.at[hop],
            device_id=(to, right),
            device_id_type=MESH,
        )

    def back_copy(out_col, hop):
        to = lax.rem(me + hop, NDATE)
        rows = pl.ds(pl.multiple_of(to * LD, LD), LD)
        return pltpu.make_async_remote_copy(
            src_ref=back.at[out_col, :, rows],
            dst_ref=home.at[me, out_col],
            send_sem=back_send.at[out_col, hop],
            recv_sem=back_recv.at[out_col, hop],
            device_id=(to, strip),
            device_id_type=MESH,
        )

    def back_local(out_col):
        return pltpu.make_async_copy(
            back.at[out_col, :, my_rows], home.at[me, out_col], back_own.at[out_col]
        )

    mask(2)
    pack_main(21, 24, 0)
    pack_tail(3, 21, 3)
    pl.semaphore_wait(barrier, 2 * NDATE - 1)
    for hop in range(NDATE):
        side_copy(hop).start()
    mask(0)
    for chunk, (_, _, (low, high), start, tails) in enumerate(CHUNKS):
        if chunk == 1:
            mask(1)
        pack_main(low, high, start)
        for tail in tails:
            pack_tail(*tail)
        for hop in range(1, NDATE):
            own_copy(chunk, hop).start()
        own_local(chunk).start()

    def pixels(block):
        return recv[block].reshape(2 * 128, WIDE)

    def tail_band(low, high):
        row = lax.broadcasted_iota(jnp.int32, (16, WIDE), 0) + (WIN - 16)
        lane = lax.broadcasted_iota(jnp.int32, (16, WIDE), 1)
        at = lane - TAIL * low
        for q in range(low + 1, high + 1):
            at = jnp.where(lane >= TAIL * q, lane - TAIL * q, at)
        at = at + WIDE
        inside = (lane >= TAIL * low) & (lane < TAIL * (high + 1))
        return jnp.where(inside & (at >= 3 * row) & (at <= 3 * row + 14), 1.0, 0.0)

    def link(out_col):
        mains = [block_of(col) for col in range(6 * out_col - 3, 6 * out_col + 4)]
        tails = [(block, tail_band(low, high)) for block, low, high in tails_of(out_col)]

        for at in range(0, 2 * 128, 32):
            part, date = at // 128, at % 128
            total = jnp.zeros((32, WIDE), jnp.float32)
            for block in mains:
                value = recv[block, part, date : date + 32, :].astype(jnp.float32)
                total = total + value * value
            high, low = split(total)
            squares[0, at : at + 32, :] = high
            squares[1, at : at + 32, :] = low
        ones = band[0:WIN, :].astype(jnp.bfloat16)
        power = dot_t(ones, squares[0]) + dot_t(ones, squares[1])
        more = jnp.zeros((16, 2 * 128), jnp.float32)
        for block, mask_ in tails:
            value = pixels(block).astype(jnp.float32)
            high, low = split(value * value)
            ones = mask_.astype(jnp.bfloat16)
            more = more + dot_t(ones, high) + dot_t(ones, low)
        power = jnp.concatenate([power[: WIN - 16], power[WIN - 16 :] + more], axis=0)
        energy = (power[:, :128] + power[:, 128:]) / NBOX + EPS
        factor = lax.rsqrt(energy)

        def sweep(step, vector):
            real, imag = vector
            real, imag = real * factor, imag * factor
            wide = jnp.concatenate(
                [
                    jnp.concatenate([real, imag], axis=1),
                    jnp.concatenate([imag, -real], axis=1),
                ],
                axis=0,
            )
            high, low = split(wide)
            total = jnp.zeros((2 * WIN, 2 * 128), jnp.float32)
            for block in mains:
                matrix = pixels(block)
                seen = (dot(high, matrix) + dot(low, matrix)) * band[...]
                seen_high, seen_low = split(seen)
                total = total + (dot_t(seen_high, matrix) + dot_t(seen_low, matrix))
            last = lambda x: jnp.concatenate([x[WIN - 16 : WIN], x[2 * WIN - 16 :]], axis=0)
            high, low = last(high), last(low)
            more = jnp.zeros((32, 2 * 128), jnp.float32)
            for block, mask_ in tails:
                matrix = pixels(block)
                seen = (dot(high, matrix) + dot(low, matrix)) * jnp.concatenate([mask_, mask_], 0)
                seen_high, seen_low = split(seen)
                more = more + (dot_t(seen_high, matrix) + dot_t(seen_low, matrix))
            first = jnp.concatenate([total[: WIN - 16], total[WIN - 16 : WIN] + more[:16]], axis=0)
            second = jnp.concatenate(
                [total[WIN : 2 * WIN - 16], total[2 * WIN - 16 :] + more[16:]], axis=0
            )
            scale = factor * (1.0 / NBOX)
            real = (first[:, :128] - second[:, 128:]) * scale
            imag = (first[:, 128:] + second[:, :128]) * scale
            size = jnp.sum(real * real + imag * imag, axis=1, keepdims=True) / 128 + EPS
            norm = lax.rsqrt(size)
            return real * norm, imag * norm

        start = (jnp.ones((WIN, 128), jnp.float32), jnp.zeros((WIN, 128), jnp.float32))
        real, imag = lax.fori_loop(0, 4, sweep, start)
        fill = jnp.zeros((128 - WIN, 128), jnp.float32)
        back[out_col, 0] = jnp.concatenate([real, fill], axis=0).T
        back[out_col, 1] = jnp.concatenate([imag, fill], axis=0).T

    for out_col in range(4):
        if out_col == 0:
            for hop in range(NDATE):
                side_copy(hop).wait_recv()

            @pl.when(strip == 0)
            def _():
                recv[0:4] = jnp.zeros((4, 2, 128, WIDE), jnp.bfloat16)

        for hop in range(1, NDATE):
            own_copy(out_col, hop).wait_recv()
        own_local(out_col).wait()
        link(out_col)
        for hop in range(1, NDATE):
            back_copy(out_col, hop).start()
        back_local(out_col).start()

    place = lax.broadcasted_iota(jnp.int32, (LD, 128), 1)
    for out_col in range(4):
        for hop in range(1, NDATE):
            back_copy(out_col, hop).wait_recv()
        back_local(out_col).wait()
        for part in range(2):
            for tile in range(6):
                k, at = tile * 128 // WIN, tile * 128 % WIN
                value = pltpu.roll(home[k, out_col, part], (-at) % 128, 1)
                done = WIN - at
                while done < 128:
                    k += 1
                    more = home[k, out_col, part]
                    if done:
                        more = pltpu.roll(more, done, 1)
                    value = jnp.where(place < done, value, more)
                    done += WIN
                out_ref[tile, pl.ds(part * (LD * 4) + out_col, LD, stride=4), :] = value

    for chunk in range(4):
        for hop in range(1, NDATE):
            own_copy(chunk, hop).wait_send()
            back_copy(chunk, hop).wait_send()
    for hop in range(NDATE):
        side_copy(hop).wait_send()


def on_device(acquisitions, valid_dates):
    dma = pltpu.SemaphoreType.DMA
    out = pl.pallas_call(
        kernel,
        name="link_phases",
        out_shape=jax.ShapeDtypeStruct((6, 2 * LD * 4, 128), jnp.float32),
        in_specs=[pl.BlockSpec(memory_space=pl.ANY)] * 2,
        out_specs=pl.BlockSpec(memory_space=pltpu.VMEM),
        scratch_shapes=[
            pltpu.VMEM((2, LD, LC, ROWS), jnp.bfloat16),
            pltpu.VMEM((LD, LC, ROWS), jnp.int32),
            pltpu.VMEM((TILES, 2 * LD * LC, 128), jnp.float32),
            pltpu.VMEM((NDATE, BLOCKS, 2, LD, WIDE), jnp.bfloat16),
            pltpu.VMEM((BLOCKS, 2, 128, WIDE), jnp.bfloat16),
            pltpu.VMEM((2, 2 * 128, WIDE), jnp.bfloat16),
            pltpu.VMEM((2 * WIN, WIDE), jnp.float32),
            pltpu.VMEM((4, 2, 128, 128), jnp.float32),
            pltpu.VMEM((NDATE, 4, 2, LD, 128), jnp.float32),
            dma((2, 3)),
            dma((4, NDATE)),
            dma((4, NDATE)),
            dma((NDATE,)),
            dma((NDATE,)),
            dma((4,)),
            dma((4, NDATE)),
            dma((4, NDATE)),
            dma((4,)),
        ],
        compiler_params=pltpu.CompilerParams(
            collective_id=0, has_side_effects=True, vmem_limit_bytes=56 << 20
        ),
    )(acquisitions, valid_dates)
    return jnp.transpose(out, (1, 0, 2)).reshape(2, LD, 4, 768)


def solution(mesh):
    in_specs = (P(None, "date", "space", None), P("date", "space", None))
    out_specs = P(None, "date", "space", None)
    return jax.shard_map(
        on_device, mesh=mesh, in_specs=in_specs, out_specs=out_specs, check_vma=False
    )
```

```python
import jax
import jax.numpy as jnp
from jax import lax
from jax.experimental import pallas as pl
from jax.experimental.pallas import tpu as pltpu
from jax.sharding import PartitionSpec as P

MESH = pl.DeviceIdType.MESH
EPS = 1e-05
NBOX = 105
NDATE = 8
NSPACE = 16
LD = 16
LC = 24
ROWS = 2304
WIN = 96
WIDE = 256
NEAR = 48
FAR = 64
LAST = 16
TAIL = 44
TILES = ROWS // 128 + 2

CHUNKS = (
    (4, 9, (0, 4), 8, 0),
    (9, 16, (4, 10), 15, 1),
    (16, 23, (10, 16), 22, 2),
    (23, 30, (16, 22), 29, 3),
)
BLOCKS = 30
USED = 22
PEERS = ((3, 1), (1, 0), (2, 1), (3, 0), (0, 1), (2, 0), (1, 1))


def block_of(col):
    if col < 0:
        return col + 3
    for first, _, (low, high), _, _ in CHUNKS:
        if low <= col < high:
            return first + col - low


def tails_of(out_col):
    low, high = 6 * out_col - 3, 6 * out_col + 3
    found = []
    if low < 0:
        found.append((3, 0, low + 3, 2))
    low = max(low, 0)
    for _, _, _, block, place in CHUNKS:
        if TAIL * low < WIDE * (place + 1) and TAIL * (high + 1) > WIDE * place:
            found.append((block, WIDE * place, low, high))
    return found


def dot(left, right):
    return lax.dot_general(
        left, right, (((1,), (0,)), ((), ())), preferred_element_type=jnp.float32
    )


def dot_t(left, right):
    return lax.dot_general(
        left, right, (((1,), (1,)), ((), ())), preferred_element_type=jnp.float32
    )


def split(value):
    high = value.astype(jnp.bfloat16)
    low = (value - high.astype(jnp.float32)).astype(jnp.bfloat16)
    return high, low


def kernel(
    acq_hbm, val_hbm, out_ref,
    acq, val, masked, send, recv, squares, near, far, linked, back, home,
    in_sem, send_sem, recv_sem, side_send, side_recv, own_sem,
    back_send, back_recv, back_own,
):
    me = lax.axis_index("date")
    strip = lax.axis_index("space")
    right = lax.rem(strip + 1, NSPACE)
    left = lax.rem(strip + NSPACE - 1, NSPACE)
    my_rows = pl.ds(pl.multiple_of(me * LD, LD), LD)

    def load(octet):
        cols = pl.ds(8 * octet, 8)
        return (
            pltpu.make_async_copy(
                acq_hbm.at[:, :, cols, :], acq.at[:, :, cols, :], in_sem.at[0, octet]
            ),
            pltpu.make_async_copy(
                val_hbm.at[:, cols, :], val.at[:, cols, :], in_sem.at[1, octet]
            ),
        )

    for octet in (2, 0, 1):
        for copy in load(octet):
            copy.start()

    barrier = pltpu.get_barrier_semaphore()
    for hop in range(1, NDATE):
        pl.semaphore_signal(
            barrier, inc=1, device_id=(lax.rem(me + hop, NDATE), strip), device_id_type=MESH
        )
    for hop in range(NDATE):
        pl.semaphore_signal(
            barrier, inc=1, device_id=(lax.rem(me + hop, NDATE), left), device_id_type=MESH
        )

    def inside(windows, first, rows):
        shape = (2 * windows, 128)
        row = lax.broadcasted_iota(jnp.int32, shape, 0)
        row = jnp.where(row >= windows, row - windows, row) + first
        at = lax.broadcasted_iota(jnp.int32, shape, 1) + rows
        return jnp.where((at >= 3 * row) & (at <= 3 * row + 14), 1.0, 0.0)

    near[...] = inside(NEAR, 0, 0)
    far[...] = inside(FAR, WIN - FAR, 128)

    masked[0] = jnp.zeros((2 * LD * LC, 128), jnp.float32)
    masked[TILES - 1] = jnp.zeros((2 * LD * LC, 128), jnp.float32)

    def mask(octet):
        for copy in load(octet):
            copy.wait()

        def body(date, carry):
            cols = pl.ds(8 * octet, 8)
            valid = val[date, cols, :].astype(jnp.float32)
            for part in range(2):
                value = acq[part, date, cols, :].astype(jnp.float32) * valid
                at = pl.multiple_of(part * (LD * LC) + date * LC + 8 * octet, 8)
                for tile in range(TILES - 2):
                    masked[1 + tile, pl.ds(at, 8), :] = value[:, tile * 128 : tile * 128 + 128]
            return carry

        lax.fori_loop(0, LD, body, 0)

    def strip_tiles(part, col, tile, count):
        at = pl.ds(part * (LD * LC) + col, LD, stride=LC)
        return jnp.concatenate([masked[tile + j, at, :] for j in range(count)], axis=1)

    def pack_main(low, high, start):
        def body(step, carry):
            col = low + step // 2
            part = step % 2
            block = start + step // 2
            for k in range(NDATE):
                at = 122 + 288 * k
                tile, shift = at // 128, at % 128
                value = strip_tiles(part, col, tile, 3)
                send[k, block, part] = value[:, shift : shift + WIDE].astype(jnp.bfloat16)
            return carry

        lax.fori_loop(0, 2 * (high - low), body, 0)

    def pack_tail(block, first, cols):
        place = lax.broadcasted_iota(jnp.int32, (LD, WIDE), 1)

        def body(part, carry):
            for k in range(NDATE):
                at = 122 + 288 * k + WIDE
                tile, shift = at // 128, at % 128
                total = jnp.zeros((LD, WIDE), jnp.float32)
                for q, col in enumerate(cols):
                    start = TAIL * q - first
                    value = strip_tiles(part, col, tile, 2)
                    moved = pltpu.roll(value, (start - shift) % WIDE, 1)
                    here = (place >= start) & (place < start + TAIL)
                    total = jnp.where(here, moved, total)
                send[k, block, part] = total.astype(jnp.bfloat16)
            return carry

        lax.fori_loop(0, 2, body, 0)

    def pack_tails(block, place):
        low, high = WIDE * place // TAIL, min((WIDE * place + WIDE - 1) // TAIL, USED - 1)
        pack_tail(block, WIDE * place - TAIL * low, range(low, high + 1))

    def peer_of(peer):
        along, other = peer
        z = lax.rem(me, 2)
        return 2 * lax.rem(me // 2 + along, NDATE // 2) + (1 - z if other else z)

    def own_copy(chunk, peer):
        low, high = CHUNKS[chunk][:2]
        to = peer_of(peer)
        hop = 2 * peer[0] + peer[1]
        return pltpu.make_async_remote_copy(
            src_ref=send.at[to, low:high],
            dst_ref=recv.at[low:high, :, my_rows],
            send_sem=send_sem.at[chunk, hop],
            recv_sem=recv_sem.at[chunk, hop],
            device_id=(to, strip),
            device_id_type=MESH,
        )

    def own_local(chunk):
        low, high = CHUNKS[chunk][:2]
        return pltpu.make_async_copy(
            send.at[me, low:high], recv.at[low:high, :, my_rows], own_sem.at[chunk]
        )

    def side_copy(hop):
        to = lax.rem(me + hop, NDATE)
        return pltpu.make_async_remote_copy(
            src_ref=send.at[to, 0:4],
            dst_ref=recv.at[0:4, :, my_rows],
            send_sem=side_send.at[hop],
            recv_sem=side_recv.at[hop],
            device_id=(to, right),
            device_id_type=MESH,
        )

    def back_copy(tile, peer):
        to = peer_of(peer)
        hop = 2 * peer[0] + peer[1]
        rows = pl.ds(pl.multiple_of(to * LD, LD), LD)
        return pltpu.make_async_remote_copy(
            src_ref=back.at[tile, :, rows],
            dst_ref=home.at[me, tile],
            send_sem=back_send.at[tile, hop],
            recv_sem=back_recv.at[tile, hop],
            device_id=(to, strip),
            device_id_type=MESH,
        )

    def back_local(tile):
        return pltpu.make_async_copy(
            back.at[tile, :, my_rows], home.at[me, tile], back_own.at[tile]
        )

    mask(2)
    pack_main(21, 24, 0)
    pack_tail(3, 0, (21, 22, 23))
    pl.semaphore_wait(barrier, 2 * NDATE - 1)
    for hop in range(NDATE):
        side_copy(hop).start()
    mask(0)
    for chunk, (start, _, (low, high), block, place) in enumerate(CHUNKS):
        if chunk == 1:
            mask(1)
        pack_main(low, high, start)
        pack_tails(block, place)
        for peer in PEERS:
            own_copy(chunk, peer).start()
        own_local(chunk).start()

    def pixels(block):
        return recv[block].reshape(2 * 128, WIDE)

    def pairs(blocks, lanes):
        one = [recv[block, :, :, lanes : lanes + 128].reshape(2 * 128, 128) for block in blocks]
        return [
            jnp.concatenate(one[j : j + 2], axis=1) if j + 1 < len(one) else one[j]
            for j in range(0, len(one), 2)
        ]

    def tail_band(first, low, high):
        row = lax.broadcasted_iota(jnp.int32, (LAST, WIDE), 0) + (WIN - LAST)
        lane = lax.broadcasted_iota(jnp.int32, (LAST, WIDE), 1) + first
        at = lane - TAIL * low
        for q in range(low + 1, high + 1):
            at = jnp.where(lane >= TAIL * q, lane - TAIL * q, at)
        at = at + WIDE
        here = (lane >= TAIL * low) & (lane < TAIL * (high + 1))
        return jnp.where(here & (at >= 3 * row) & (at <= 3 * row + 14), 1.0, 0.0)

    def merge(first, second, third):
        both = first[WIN - FAR :] + second[: NEAR + FAR - WIN]
        middle = second[NEAR + FAR - WIN : FAR - LAST]
        end = second[FAR - LAST :] + third
        return jnp.concatenate([first[: WIN - FAR], both, middle, end], axis=0)

    def link(out_col):
        mains = [block_of(col) for col in range(6 * out_col - 3, 6 * out_col + 4)]
        tails = [
            (block, tail_band(first, low, high))
            for block, first, low, high in tails_of(out_col)
        ]

        for at in range(0, 2 * 128, 32):
            part, date = at // 128, at % 128
            total = jnp.zeros((32, WIDE), jnp.float32)
            for block in mains:
                value = recv[block, part, date : date + 32, :].astype(jnp.float32)
                total = total + value * value
            high, low = split(total)
            squares[0, at : at + 32, :] = high
            squares[1, at : at + 32, :] = low

        def power(ones, lanes):
            lanes = slice(lanes, lanes + 128)
            return dot_t(ones, squares[0, :, lanes]) + dot_t(ones, squares[1, :, lanes])

        last = jnp.zeros((LAST, 2 * 128), jnp.float32)
        for block, ones in tails:
            value = pixels(block).astype(jnp.float32)
            high, low = split(value * value)
            ones = ones.astype(jnp.bfloat16)
            last = last + dot_t(ones, high) + dot_t(ones, low)
        energy = merge(
            power(near[:NEAR].astype(jnp.bfloat16), 0),
            power(far[:FAR].astype(jnp.bfloat16), 128),
            last,
        )
        energy = (energy[:, :128] + energy[:, 128:]) / NBOX + EPS
        factor = lax.rsqrt(energy)

        def back_and_forth(wide, matrices, bands):
            high, low = split(wide)
            total = None
            for matrix, ones in zip(matrices, bands):
                if ones.shape[1] < matrix.shape[1]:
                    ones = jnp.concatenate([ones, ones], axis=1)
                seen = (dot(high, matrix) + dot(low, matrix)) * ones
                seen_high, seen_low = split(seen)
                more = dot_t(seen_high, matrix) + dot_t(seen_low, matrix)
                total = more if total is None else total + more
            return total

        def sweep(step, vector):
            real, imag = vector
            real, imag = real * factor, imag * factor
            upper = jnp.concatenate([real, imag], axis=1)
            lower = jnp.concatenate([imag, -real], axis=1)
            stack = lambda low, high: jnp.concatenate([upper[low:high], lower[low:high]], axis=0)
            first = back_and_forth(stack(0, NEAR), pairs(mains, 0), [near[...]] * 4)
            second = back_and_forth(stack(WIN - FAR, WIN), pairs(mains, 128), [far[...]] * 4)
            third = back_and_forth(
                stack(WIN - LAST, WIN),
                [pixels(block) for block, _ in tails],
                [jnp.concatenate([ones, ones], axis=0) for _, ones in tails],
            )
            upper = merge(first[:NEAR], second[:FAR], third[:LAST])
            lower = merge(first[NEAR:], second[FAR:], third[LAST:])
            scale = factor * (1.0 / NBOX)
            real = (upper[:, :128] - lower[:, 128:]) * scale
            imag = (upper[:, 128:] + lower[:, :128]) * scale
            size = jnp.sum(real * real + imag * imag, axis=1, keepdims=True) / 128 + EPS
            norm = lax.rsqrt(size)
            return real * norm, imag * norm

        start = (jnp.ones((WIN, 128), jnp.float32), jnp.zeros((WIN, 128), jnp.float32))
        real, imag = lax.fori_loop(0, 4, sweep, start)
        linked[0, out_col * WIN : out_col * WIN + WIN] = real
        linked[1, out_col * WIN : out_col * WIN + WIN] = imag

    def send_back(tile):
        for part in range(2):
            back[tile, part] = linked[part, tile * 128 : tile * 128 + 128].T
        for peer in PEERS:
            back_copy(tile, peer).start()
        back_local(tile).start()

    place = lax.broadcasted_iota(jnp.int32, (LD, 128), 1)

    def assemble(out_col, part, tile):
        value = None
        done = 0
        while done < 128:
            k, window = (tile * 128 + done) // WIN, (tile * 128 + done) % WIN
            source, lane = (out_col * WIN + window) // 128, (out_col * WIN + window) % 128
            more = home[k, source, part]
            if lane != done:
                more = pltpu.roll(more, (done - lane) % 128, 1)
            value = more if value is None else jnp.where(place < done, value, more)
            done += min(WIN - window, 128 - lane, 128 - done)
        out_ref[part, :, out_col, tile * 128 : tile * 128 + 128] = value

    for out_col in range(4):
        if out_col == 0:
            for hop in range(NDATE):
                side_copy(hop).wait_recv()

            @pl.when(strip == 0)
            def _():
                recv[0:4] = jnp.zeros((4, 2, 128, WIDE), jnp.bfloat16)

        for peer in PEERS:
            own_copy(out_col, peer).wait_recv()
        own_local(out_col).wait()
        link(out_col)
        if out_col:
            send_back(out_col - 1)

    for source in range(3):
        for peer in PEERS:
            back_copy(source, peer).wait_recv()
        back_local(source).wait()
        for out_col in ((0,), (1,), (2, 3))[source]:
            for part in range(2):
                for tile in range(6):
                    assemble(out_col, part, tile)

    for peer in PEERS:
        for chunk in range(4):
            own_copy(chunk, peer).wait_send()
        for tile in range(3):
            back_copy(tile, peer).wait_send()
    for hop in range(NDATE):
        side_copy(hop).wait_send()


def on_device(acquisitions, valid_dates):
    dma = pltpu.SemaphoreType.DMA
    return pl.pallas_call(
        kernel,
        name="link_phases",
        out_shape=jax.ShapeDtypeStruct((2, LD, 4, 768), jnp.float32),
        in_specs=[pl.BlockSpec(memory_space=pl.ANY)] * 2,
        out_specs=pl.BlockSpec(memory_space=pltpu.VMEM),
        scratch_shapes=[
            pltpu.VMEM((2, LD, LC, ROWS), jnp.bfloat16),
            pltpu.VMEM((LD, LC, ROWS), jnp.int32),
            pltpu.VMEM((TILES, 2 * LD * LC, 128), jnp.float32),
            pltpu.VMEM((NDATE, BLOCKS, 2, LD, WIDE), jnp.bfloat16),
            pltpu.VMEM((BLOCKS, 2, 128, WIDE), jnp.bfloat16),
            pltpu.VMEM((2, 2 * 128, WIDE), jnp.bfloat16),
            pltpu.VMEM((2 * NEAR, 128), jnp.float32),
            pltpu.VMEM((2 * FAR, 128), jnp.float32),
            pltpu.VMEM((2, 4 * WIN, 128), jnp.float32),
            pltpu.VMEM((3, 2, 128, 128), jnp.float32),
            pltpu.VMEM((NDATE, 3, 2, LD, 128), jnp.float32),
            dma((2, 3)),
            dma((4, NDATE)),
            dma((4, NDATE)),
            dma((NDATE,)),
            dma((NDATE,)),
            dma((4,)),
            dma((3, NDATE)),
            dma((3, NDATE)),
            dma((3,)),
        ],
        compiler_params=pltpu.CompilerParams(
            collective_id=0, has_side_effects=True, vmem_limit_bytes=56 << 20
        ),
    )(acquisitions, valid_dates)


def solution(mesh):
    in_specs = (P(None, "date", "space", None), P("date", "space", None))
    out_specs = P(None, "date", "space", None)
    return jax.shard_map(
        on_device, mesh=mesh, in_specs=in_specs, out_specs=out_specs, check_vma=False
    )
```

```python
import jax
import jax.numpy as jnp
from jax import lax
from jax.experimental import pallas as pl
from jax.experimental.pallas import tpu as pltpu
from jax.sharding import PartitionSpec as P

MESH = pl.DeviceIdType.MESH
EPS = 1e-05
NBOX = 105
NDATE = 8
NSPACE = 16
LD = 16
LC = 24
ROWS = 2304
WIN = 96
WIDE = 256
NEAR = 48
FAR = 64
LAST = 16
TAIL = 44
TILES = ROWS // 128 + 2

CHUNKS = (
    (4, 9, (0, 4), 8, 0),
    (9, 16, (4, 10), 15, 1),
    (16, 23, (10, 16), 22, 2),
    (23, 30, (16, 22), 29, 3),
)
BLOCKS = 30
USED = 22
PEERS = ((3, 1), (1, 0), (2, 1), (3, 0), (0, 1), (2, 0), (1, 1))


def block_of(col):
    if col < 0:
        return col + 3
    for first, _, (low, high), _, _ in CHUNKS:
        if low <= col < high:
            return first + col - low


def tails_of(out_col):
    low, high = 6 * out_col - 3, 6 * out_col + 3
    found = []
    if low < 0:
        found.append((3, 0, low + 3, 2))
    low = max(low, 0)
    for _, _, _, block, place in CHUNKS:
        if TAIL * low < WIDE * (place + 1) and TAIL * (high + 1) > WIDE * place:
            found.append((block, WIDE * place, low, high))
    return found


def dot(left, right):
    return lax.dot_general(
        left, right, (((1,), (0,)), ((), ())), preferred_element_type=jnp.float32
    )


def dot_t(left, right):
    return lax.dot_general(
        left, right, (((1,), (1,)), ((), ())), preferred_element_type=jnp.float32
    )


def split(value):
    high = value.astype(jnp.bfloat16)
    low = (value - high.astype(jnp.float32)).astype(jnp.bfloat16)
    return high, low


def kernel(
    acq_hbm, val_hbm, out_ref,
    acq, val, masked, send, recv, squares, near, far, linked, back, home,
    in_sem, send_sem, recv_sem, side_send, side_recv, own_sem,
    back_send, back_recv, back_own,
):
    me = lax.axis_index("date")
    strip = lax.axis_index("space")
    right = lax.rem(strip + 1, NSPACE)
    left = lax.rem(strip + NSPACE - 1, NSPACE)
    my_rows = pl.ds(pl.multiple_of(me * LD, LD), LD)

    def load(octet):
        cols = pl.ds(8 * octet, 8)
        return (
            pltpu.make_async_copy(
                acq_hbm.at[:, :, cols, :], acq.at[:, :, cols, :], in_sem.at[0, octet]
            ),
            pltpu.make_async_copy(
                val_hbm.at[:, cols, :], val.at[:, cols, :], in_sem.at[1, octet]
            ),
        )

    for octet in (2, 0, 1):
        for copy in load(octet):
            copy.start()

    barrier = pltpu.get_barrier_semaphore()
    for hop in range(1, NDATE):
        pl.semaphore_signal(
            barrier, inc=1, device_id=(lax.rem(me + hop, NDATE), strip), device_id_type=MESH
        )
    for hop in range(NDATE):
        pl.semaphore_signal(
            barrier, inc=1, device_id=(lax.rem(me + hop, NDATE), left), device_id_type=MESH
        )

    def inside(windows, first, rows):
        shape = (2 * windows, 128)
        row = lax.broadcasted_iota(jnp.int32, shape, 0)
        row = jnp.where(row >= windows, row - windows, row) + first
        at = lax.broadcasted_iota(jnp.int32, shape, 1) + rows
        return jnp.where((at >= 3 * row) & (at <= 3 * row + 14), 1.0, 0.0)

    near[...] = inside(NEAR, 0, 0)
    far[...] = inside(FAR, WIN - FAR, 128)

    masked[0] = jnp.zeros((2 * LD * LC, 128), jnp.float32)
    masked[TILES - 1] = jnp.zeros((2 * LD * LC, 128), jnp.float32)

    def mask(octet):
        for copy in load(octet):
            copy.wait()

        def body(date, carry):
            cols = pl.ds(8 * octet, 8)
            valid = val[date, cols, :].astype(jnp.float32)
            for part in range(2):
                value = acq[part, date, cols, :].astype(jnp.float32) * valid
                at = pl.multiple_of(part * (LD * LC) + date * LC + 8 * octet, 8)
                for tile in range(TILES - 2):
                    masked[1 + tile, pl.ds(at, 8), :] = value[:, tile * 128 : tile * 128 + 128]
            return carry

        lax.fori_loop(0, LD, body, 0)

    def strip_tiles(part, col, tile, count):
        at = pl.ds(part * (LD * LC) + col, LD, stride=LC)
        return jnp.concatenate([masked[tile + j, at, :] for j in range(count)], axis=1)

    def pack_main(low, high, start):
        def body(step, carry):
            col = low + step // 2
            part = step % 2
            block = start + step // 2
            for k in range(NDATE):
                at = 122 + 288 * k
                tile, shift = at // 128, at % 128
                value = strip_tiles(part, col, tile, 3)
                send[k, block, part] = value[:, shift : shift + WIDE].astype(jnp.bfloat16)
            return carry

        lax.fori_loop(0, 2 * (high - low), body, 0)

    def pack_tail(block, first, cols):
        place = lax.broadcasted_iota(jnp.int32, (LD, WIDE), 1)

        def body(part, carry):
            for k in range(NDATE):
                at = 122 + 288 * k + WIDE
                tile, shift = at // 128, at % 128
                total = jnp.zeros((LD, WIDE), jnp.float32)
                for q, col in enumerate(cols):
                    start = TAIL * q - first
                    value = strip_tiles(part, col, tile, 2)
                    moved = pltpu.roll(value, (start - shift) % WIDE, 1)
                    here = (place >= start) & (place < start + TAIL)
                    total = jnp.where(here, moved, total)
                send[k, block, part] = total.astype(jnp.bfloat16)
            return carry

        lax.fori_loop(0, 2, body, 0)

    def pack_tails(block, place):
        low, high = WIDE * place // TAIL, min((WIDE * place + WIDE - 1) // TAIL, USED - 1)
        pack_tail(block, WIDE * place - TAIL * low, range(low, high + 1))

    def peer_of(peer):
        along, other = peer
        z = lax.rem(me, 2)
        return 2 * lax.rem(me // 2 + along, NDATE // 2) + (1 - z if other else z)

    def own_copy(chunk, peer):
        low, high = CHUNKS[chunk][:2]
        to = peer_of(peer)
        hop = 2 * peer[0] + peer[1]
        return pltpu.make_async_remote_copy(
            src_ref=send.at[to, low:high],
            dst_ref=recv.at[low:high, :, my_rows],
            send_sem=send_sem.at[chunk, hop],
            recv_sem=recv_sem.at[chunk, hop],
            device_id=(to, strip),
            device_id_type=MESH,
        )

    def own_local(chunk):
        low, high = CHUNKS[chunk][:2]
        return pltpu.make_async_copy(
            send.at[me, low:high], recv.at[low:high, :, my_rows], own_sem.at[chunk]
        )

    def side_copy(hop):
        to = lax.rem(me + hop, NDATE)
        return pltpu.make_async_remote_copy(
            src_ref=send.at[to, 0:4],
            dst_ref=recv.at[0:4, :, my_rows],
            send_sem=side_send.at[hop],
            recv_sem=side_recv.at[hop],
            device_id=(to, right),
            device_id_type=MESH,
        )

    def back_copy(tile, peer):
        to = peer_of(peer)
        hop = 2 * peer[0] + peer[1]
        rows = pl.ds(pl.multiple_of(to * LD, LD), LD)
        return pltpu.make_async_remote_copy(
            src_ref=back.at[tile, :, rows],
            dst_ref=home.at[me, tile],
            send_sem=back_send.at[tile, hop],
            recv_sem=back_recv.at[tile, hop],
            device_id=(to, strip),
            device_id_type=MESH,
        )

    def back_local(tile):
        return pltpu.make_async_copy(
            back.at[tile, :, my_rows], home.at[me, tile], back_own.at[tile]
        )

    mask(2)
    pack_main(21, 24, 0)
    pack_tail(3, 0, (21, 22, 23))
    pl.semaphore_wait(barrier, 2 * NDATE - 1)
    for hop in range(NDATE):
        side_copy(hop).start()
    mask(0)
    for chunk, (start, _, (low, high), block, place) in enumerate(CHUNKS):
        if chunk == 1:
            mask(1)
        pack_main(low, high, start)
        pack_tails(block, place)
        for peer in PEERS:
            own_copy(chunk, peer).start()
        own_local(chunk).start()

    def pixels(block):
        return recv[block].reshape(2 * 128, WIDE)

    def pairs(blocks, lanes):
        one = [recv[block, :, :, lanes : lanes + 128].reshape(2 * 128, 128) for block in blocks]
        return [
            jnp.concatenate(one[j : j + 2], axis=1) if j + 1 < len(one) else one[j]
            for j in range(0, len(one), 2)
        ]

    def tail_band(first, low, high):
        row = lax.broadcasted_iota(jnp.int32, (LAST, WIDE), 0) + (WIN - LAST)
        lane = lax.broadcasted_iota(jnp.int32, (LAST, WIDE), 1) + first
        at = lane - TAIL * low
        for q in range(low + 1, high + 1):
            at = jnp.where(lane >= TAIL * q, lane - TAIL * q, at)
        at = at + WIDE
        here = (lane >= TAIL * low) & (lane < TAIL * (high + 1))
        return jnp.where(here & (at >= 3 * row) & (at <= 3 * row + 14), 1.0, 0.0)

    def merge(first, second, third):
        both = first[WIN - FAR :] + second[: NEAR + FAR - WIN]
        middle = second[NEAR + FAR - WIN : FAR - LAST]
        end = second[FAR - LAST :] + third
        return jnp.concatenate([first[: WIN - FAR], both, middle, end], axis=0)

    def link(out_col):
        mains = [block_of(col) for col in range(6 * out_col - 3, 6 * out_col + 4)]
        tails = [
            (block, tail_band(first, low, high))
            for block, first, low, high in tails_of(out_col)
        ]

        for at in range(0, 2 * 128, 32):
            part, date = at // 128, at % 128
            total = jnp.zeros((32, WIDE), jnp.float32)
            for block in mains:
                value = recv[block, part, date : date + 32, :].astype(jnp.float32)
                total = total + value * value
            high, low = split(total)
            squares[0, at : at + 32, :] = high
            squares[1, at : at + 32, :] = low

        def power(ones, lanes):
            lanes = slice(lanes, lanes + 128)
            return dot_t(ones, squares[0, :, lanes]) + dot_t(ones, squares[1, :, lanes])

        last = jnp.zeros((LAST, 2 * 128), jnp.float32)
        for block, ones in tails:
            value = pixels(block).astype(jnp.float32)
            high, low = split(value * value)
            ones = ones.astype(jnp.bfloat16)
            last = last + dot_t(ones, high) + dot_t(ones, low)
        energy = merge(
            power(near[:NEAR].astype(jnp.bfloat16), 0),
            power(far[:FAR].astype(jnp.bfloat16), 128),
            last,
        )
        energy = (energy[:, :128] + energy[:, 128:]) / NBOX + EPS
        factor = lax.rsqrt(energy)

        def back_and_forth(wide, matrices, bands):
            count = wide.shape[0]
            wide = jnp.concatenate(split(wide), axis=0)
            total = None
            for matrix, ones in zip(matrices, bands):
                if ones.shape[1] < matrix.shape[1]:
                    ones = jnp.concatenate([ones, ones], axis=1)
                seen = dot(wide, matrix)
                seen = (seen[:count] + seen[count:]) * ones
                more = dot_t(jnp.concatenate(split(seen), axis=0), matrix)
                total = more if total is None else total + more
            return total[:count] + total[count:]

        def sweep(step, vector):
            real, imag = vector
            real, imag = real * factor, imag * factor
            upper = jnp.concatenate([real, imag], axis=1)
            lower = jnp.concatenate([imag, -real], axis=1)
            stack = lambda low, high: jnp.concatenate([upper[low:high], lower[low:high]], axis=0)
            first = back_and_forth(stack(0, NEAR), pairs(mains, 0), [near[...]] * 4)
            second = back_and_forth(stack(WIN - FAR, WIN), pairs(mains, 128), [far[...]] * 4)
            third = back_and_forth(
                stack(WIN - LAST, WIN),
                [pixels(block) for block, _ in tails],
                [jnp.concatenate([ones, ones], axis=0) for _, ones in tails],
            )
            upper = merge(first[:NEAR], second[:FAR], third[:LAST])
            lower = merge(first[NEAR:], second[FAR:], third[LAST:])
            scale = factor * (1.0 / NBOX)
            real = (upper[:, :128] - lower[:, 128:]) * scale
            imag = (upper[:, 128:] + lower[:, :128]) * scale
            size = jnp.sum(real * real + imag * imag, axis=1, keepdims=True) / 128 + EPS
            norm = lax.rsqrt(size)
            return real * norm, imag * norm

        start = (jnp.ones((WIN, 128), jnp.float32), jnp.zeros((WIN, 128), jnp.float32))
        real, imag = lax.fori_loop(0, 4, sweep, start)
        linked[0, out_col * WIN : out_col * WIN + WIN] = real
        linked[1, out_col * WIN : out_col * WIN + WIN] = imag

    def send_back(tile):
        for part in range(2):
            back[tile, part] = linked[part, tile * 128 : tile * 128 + 128].T
        for peer in PEERS:
            back_copy(tile, peer).start()
        back_local(tile).start()

    place = lax.broadcasted_iota(jnp.int32, (LD, 128), 1)

    def assemble(out_col, part, tile):
        value = None
        done = 0
        while done < 128:
            k, window = (tile * 128 + done) // WIN, (tile * 128 + done) % WIN
            source, lane = (out_col * WIN + window) // 128, (out_col * WIN + window) % 128
            more = home[k, source, part]
            if lane != done:
                more = pltpu.roll(more, (done - lane) % 128, 1)
            value = more if value is None else jnp.where(place < done, value, more)
            done += min(WIN - window, 128 - lane, 128 - done)
        out_ref[part, :, out_col, tile * 128 : tile * 128 + 128] = value

    for out_col in range(4):
        if out_col == 0:
            for hop in range(NDATE):
                side_copy(hop).wait_recv()

            @pl.when(strip == 0)
            def _():
                recv[0:4] = jnp.zeros((4, 2, 128, WIDE), jnp.bfloat16)

        for peer in PEERS:
            own_copy(out_col, peer).wait_recv()
        own_local(out_col).wait()
        link(out_col)
        if out_col:
            send_back(out_col - 1)

    for source in range(3):
        for peer in PEERS:
            back_copy(source, peer).wait_recv()
        back_local(source).wait()
        for out_col in ((0,), (1,), (2, 3))[source]:
            for part in range(2):
                for tile in range(6):
                    assemble(out_col, part, tile)

    for peer in PEERS:
        for chunk in range(4):
            own_copy(chunk, peer).wait_send()
        for tile in range(3):
            back_copy(tile, peer).wait_send()
    for hop in range(NDATE):
        side_copy(hop).wait_send()


def on_device(acquisitions, valid_dates):
    dma = pltpu.SemaphoreType.DMA
    return pl.pallas_call(
        kernel,
        name="link_phases",
        out_shape=jax.ShapeDtypeStruct((2, LD, 4, 768), jnp.float32),
        in_specs=[pl.BlockSpec(memory_space=pl.ANY)] * 2,
        out_specs=pl.BlockSpec(memory_space=pltpu.VMEM),
        scratch_shapes=[
            pltpu.VMEM((2, LD, LC, ROWS), jnp.bfloat16),
            pltpu.VMEM((LD, LC, ROWS), jnp.int32),
            pltpu.VMEM((TILES, 2 * LD * LC, 128), jnp.float32),
            pltpu.VMEM((NDATE, BLOCKS, 2, LD, WIDE), jnp.bfloat16),
            pltpu.VMEM((BLOCKS, 2, 128, WIDE), jnp.bfloat16),
            pltpu.VMEM((2, 2 * 128, WIDE), jnp.bfloat16),
            pltpu.VMEM((2 * NEAR, 128), jnp.float32),
            pltpu.VMEM((2 * FAR, 128), jnp.float32),
            pltpu.VMEM((2, 4 * WIN, 128), jnp.float32),
            pltpu.VMEM((3, 2, 128, 128), jnp.float32),
            pltpu.VMEM((NDATE, 3, 2, LD, 128), jnp.float32),
            dma((2, 3)),
            dma((4, NDATE)),
            dma((4, NDATE)),
            dma((NDATE,)),
            dma((NDATE,)),
            dma((4,)),
            dma((3, NDATE)),
            dma((3, NDATE)),
            dma((3,)),
        ],
        compiler_params=pltpu.CompilerParams(
            collective_id=0, has_side_effects=True, vmem_limit_bytes=56 << 20
        ),
    )(acquisitions, valid_dates)


def solution(mesh):
    in_specs = (P(None, "date", "space", None), P("date", "space", None))
    out_specs = P(None, "date", "space", None)
    return jax.shard_map(
        on_device, mesh=mesh, in_specs=in_specs, out_specs=out_specs, check_vma=False
    )
```

```python
import jax
import jax.numpy as jnp
from jax import lax
from jax.experimental import pallas as pl
from jax.experimental.pallas import tpu as pltpu
from jax.sharding import PartitionSpec as P

MESH = pl.DeviceIdType.MESH
EPS = 1e-05
NBOX = 105
NDATE = 8
NSPACE = 16
LD = 16
LC = 24
ROWS = 2304
WIN = 96
WIDE = 256
NEAR = 48
FAR = 64
LAST = 16
TAIL = 44
TILES = ROWS // 128 + 2

CHUNKS = (
    (4, 9, (0, 4), 8, 0),
    (9, 16, (4, 10), 15, 1),
    (16, 23, (10, 16), 22, 2),
    (23, 30, (16, 22), 29, 3),
)
BLOCKS = 30
CODE = 7.5
USED = 22
ORDER = 5
PEERS = range(1, NDATE)


def block_of(col):
    if col < 0:
        return col + 3
    for first, _, (low, high), _, _ in CHUNKS:
        if low <= col < high:
            return first + col - low


def tails_of(out_col):
    low, high = 6 * out_col - 3, 6 * out_col + 3
    found = []
    if low < 0:
        found.append((3, 0, low + 3, 2))
    low = max(low, 0)
    for _, _, _, block, place in CHUNKS:
        if TAIL * low < WIDE * (place + 1) and TAIL * (high + 1) > WIDE * place:
            found.append((block, WIDE * place, low, high))
    return found


def dot(left, right):
    return lax.dot_general(
        left, right, (((1,), (0,)), ((), ())), preferred_element_type=jnp.float32
    )


def dot_t(left, right):
    return lax.dot_general(
        left, right, (((1,), (1,)), ((), ())), preferred_element_type=jnp.float32
    )


def split(value):
    high = value.astype(jnp.bfloat16)
    low = (value - high.astype(jnp.float32)).astype(jnp.bfloat16)
    return high, low


def kernel(
    acq_hbm, val_hbm, out_ref,
    acq, val, masked, send, recv, squares, near, far, linked, back, home,
    in_sem, send_sem, recv_sem, side_send, side_recv, own_sem,
    back_send, back_recv, back_own,
):
    me = lax.axis_index("date")
    strip = lax.axis_index("space")
    right = lax.rem(strip + 1, NSPACE)
    left = lax.rem(strip + NSPACE - 1, NSPACE)
    my_rows = pl.ds(pl.multiple_of(me * LD, LD), LD)

    def load(octet):
        cols = pl.ds(8 * octet, 8)
        return (
            pltpu.make_async_copy(
                acq_hbm.at[:, :, cols, :], acq.at[:, :, cols, :], in_sem.at[0, octet]
            ),
            pltpu.make_async_copy(
                val_hbm.at[:, cols, :], val.at[:, cols, :], in_sem.at[1, octet]
            ),
        )

    for copy in load(2):
        copy.start()

    barrier = pltpu.get_barrier_semaphore()
    for hop in range(1, NDATE):
        pl.semaphore_signal(
            barrier, inc=1, device_id=(lax.rem(me + hop, NDATE), strip), device_id_type=MESH
        )
    for hop in range(NDATE):
        pl.semaphore_signal(
            barrier, inc=1, device_id=(lax.rem(me + hop, NDATE), left), device_id_type=MESH
        )

    def inside(windows, first, rows):
        shape = (2 * windows, 128)
        row = lax.broadcasted_iota(jnp.int32, shape, 0)
        row = jnp.where(row >= windows, row - windows, row) + first
        at = lax.broadcasted_iota(jnp.int32, shape, 1) + rows
        return jnp.where((at >= 3 * row) & (at <= 3 * row + 14), 1.0, 0.0)

    near[...] = inside(NEAR, 0, 0)
    far[...] = inside(FAR, WIN - FAR, 128)

    masked[0] = jnp.zeros((2 * LD * LC, 128), jnp.float32)
    masked[TILES - 1] = jnp.zeros((2 * LD * LC, 128), jnp.float32)

    def mask(octet):
        if octet < 2:
            for copy in load(octet):
                copy.wait()

        def body(date, carry):
            cols = pl.ds(8 * octet, 8)
            valid = val[date, cols, :].astype(jnp.float32)
            for part in range(2):
                value = acq[part, date, cols, :].astype(jnp.float32) * valid
                at = pl.multiple_of(part * (LD * LC) + date * LC + 8 * octet, 8)
                for tile in range(TILES - 2):
                    masked[1 + tile, pl.ds(at, 8), :] = value[:, tile * 128 : tile * 128 + 128]
            return carry

        lax.fori_loop(0, LD, body, 0)

    def hop_of(turn):
        return lax.rem(ORDER * turn, NDATE)

    def peer_of(turn):
        hop = hop_of(turn)
        z = lax.rem(me, 2)
        return 2 * lax.rem(me // 2 + hop // 2, NDATE // 2) + lax.rem(z + hop, 2)

    def mask_for(octet, k):
        first = (122 + 288 * k) // 128

        def body(date, carry):
            cols = pl.ds(8 * octet, 8)
            for j in range(4):
                tile = jnp.clip(first + j, 1, TILES - 2)
                rows = pl.ds(pl.multiple_of((tile - 1) * 128, 128), 128)
                valid = val[date, cols, rows].astype(jnp.float32)
                for part in range(2):
                    value = acq[part, date, cols, rows].astype(jnp.float32) * valid
                    at = pl.multiple_of(part * (LD * LC) + date * LC + 8 * octet, 8)
                    masked[tile, pl.ds(at, 8), :] = value
            return carry

        lax.fori_loop(0, LD, body, 0, unroll=4)

    spot = lax.broadcasted_iota(jnp.int32, (LD, 128), 1)

    def turned(part, col, k, skip, count):
        first = 122 + 288 * k
        tile = first // 128
        rest = 128 - (first - tile * 128)
        at = pl.ds(part * (LD * LC) + col, LD, stride=LC)
        raw = [pltpu.roll(masked[tile + skip + j, at, :], rest, 1) for j in range(count + 1)]
        return [jnp.where(spot < rest, raw[j], raw[j + 1]) for j in range(count)]

    def pack_main(k, low, high, start):
        for col in range(low, high):
            for part in range(2):
                value = jnp.concatenate(turned(part, col, k, 0, 2), axis=1)
                send[k, start + col - low, part] = value.astype(jnp.bfloat16)

    def pack_tail(k, block, first, cols):
        for part in range(2):
            halves = [jnp.zeros((LD, 128), jnp.float32)] * 2
            for q, col in enumerate(cols):
                value = turned(part, col, k, 2, 1)[0]
                for half in range(2):
                    start = TAIL * q - first - 128 * half
                    if -TAIL < start < 128:
                        moved = pltpu.roll(value, start % 128, 1) if start % 128 else value
                        here = (spot >= start) & (spot < start + TAIL)
                        halves[half] = jnp.where(here, moved, halves[half])
            send[k, block, part] = jnp.concatenate(halves, axis=1).astype(jnp.bfloat16)

    def pack_tails(k, block, place):
        low, high = WIDE * place // TAIL, min((WIDE * place + WIDE - 1) // TAIL, USED - 1)
        pack_tail(k, block, WIDE * place - TAIL * low, range(low, high + 1))

    def own_copy(chunk, peer):
        low, high = CHUNKS[chunk][:2]
        to = peer_of(peer)
        hop = hop_of(peer)
        return pltpu.make_async_remote_copy(
            src_ref=send.at[to, low:high],
            dst_ref=recv.at[low:high, :, my_rows],
            send_sem=send_sem.at[chunk, hop],
            recv_sem=recv_sem.at[chunk, hop],
            device_id=(to, strip),
            device_id_type=MESH,
        )

    def own_local(chunk):
        low, high = CHUNKS[chunk][:2]
        return pltpu.make_async_copy(
            send.at[me, low:high], recv.at[low:high, :, my_rows], own_sem.at[chunk]
        )

    def side_copy(peer):
        to = peer_of(peer)
        hop = hop_of(peer)
        return pltpu.make_async_remote_copy(
            src_ref=send.at[to, 0:4],
            dst_ref=recv.at[0:4, :, my_rows],
            send_sem=side_send.at[hop],
            recv_sem=side_recv.at[hop],
            device_id=(to, right),
            device_id_type=MESH,
        )

    def back_copy(tile, peer):
        to = peer_of(peer)
        hop = hop_of(peer)
        rows = pl.ds(pl.multiple_of(to * LD, LD), LD)
        return pltpu.make_async_remote_copy(
            src_ref=back.at[tile, :, rows],
            dst_ref=home.at[me, tile],
            send_sem=back_send.at[tile, hop],
            recv_sem=back_recv.at[tile, hop],
            device_id=(to, strip),
            device_id_type=MESH,
        )

    def back_local(tile):
        return pltpu.make_async_copy(
            back.at[tile, :, my_rows], home.at[me, tile], back_own.at[tile]
        )

    for copy in load(2):
        copy.wait()
    for octet in range(2):
        for copy in load(octet):
            copy.start()

    def fill_side(turn):
        to = peer_of(turn)
        pack_main(to, 21, 24, 0)
        pack_tail(to, 3, 0, (21, 22, 23))

    def send_side(turn, carry):
        fill_side(turn)
        side_copy(turn).start()
        return carry

    mask_for(2, peer_of(1))
    fill_side(1)
    pl.semaphore_wait(barrier, 2 * NDATE - 1)
    side_copy(1).start()
    mask(2)
    lax.fori_loop(2, NDATE + 1, send_side, 0)
    mask(0)
    for chunk, (start, _, (low, high), block, place) in enumerate(CHUNKS):
        if chunk == 1:
            mask(1)

        def send_own(turn, carry):
            to = peer_of(turn)
            pack_main(to, low, high, start)
            pack_tails(to, block, place)

            @pl.when(turn < NDATE)
            def _():
                own_copy(chunk, turn).start()

            return carry

        lax.fori_loop(1, NDATE + 1, send_own, 0)
        own_local(chunk).start()

    def pixels(block):
        return recv[block].reshape(2 * 128, WIDE)

    def pairs(blocks, lanes):
        one = [recv[block, :, :, lanes : lanes + 128].reshape(2 * 128, 128) for block in blocks]
        return [
            jnp.concatenate(one[j : j + 2], axis=1) if j + 1 < len(one) else one[j]
            for j in range(0, len(one), 2)
        ]

    def tail_band(first, low, high):
        row = lax.broadcasted_iota(jnp.int32, (LAST, WIDE), 0) + (WIN - LAST)
        lane = lax.broadcasted_iota(jnp.int32, (LAST, WIDE), 1) + first
        at = lane - TAIL * low
        for q in range(low + 1, high + 1):
            at = jnp.where(lane >= TAIL * q, lane - TAIL * q, at)
        at = at + WIDE
        here = (lane >= TAIL * low) & (lane < TAIL * (high + 1))
        return jnp.where(here & (at >= 3 * row) & (at <= 3 * row + 14), 1.0, 0.0)

    def merge(first, second, third):
        both = first[WIN - FAR :] + second[: NEAR + FAR - WIN]
        middle = second[NEAR + FAR - WIN : FAR - LAST]
        end = second[FAR - LAST :] + third
        return jnp.concatenate([first[: WIN - FAR], both, middle, end], axis=0)

    def link(out_col):
        mains = [block_of(col) for col in range(6 * out_col - 3, 6 * out_col + 4)]
        tails = [
            (block, tail_band(first, low, high))
            for block, first, low, high in tails_of(out_col)
        ]

        for at in range(0, 2 * 128, 32):
            part, date = at // 128, at % 128
            total = jnp.zeros((32, WIDE), jnp.float32)
            for block in mains:
                value = recv[block, part, date : date + 32, :].astype(jnp.float32)
                total = total + value * value
            high, low = split(total)
            squares[0, at : at + 32, :] = high
            squares[1, at : at + 32, :] = low

        def power(ones, lanes):
            lanes = slice(lanes, lanes + 128)
            return dot_t(ones, squares[0, :, lanes]) + dot_t(ones, squares[1, :, lanes])

        last = jnp.zeros((LAST, 2 * 128), jnp.float32)
        for block, ones in tails:
            value = pixels(block).astype(jnp.float32)
            high, low = split(value * value)
            ones = ones.astype(jnp.bfloat16)
            last = last + dot_t(ones, high) + dot_t(ones, low)
        energy = merge(
            power(near[:NEAR].astype(jnp.bfloat16), 0),
            power(far[:FAR].astype(jnp.bfloat16), 128),
            last,
        )
        energy = (energy[:, :128] + energy[:, 128:]) / NBOX + EPS
        factor = lax.rsqrt(energy)

        def back_and_forth(wide, matrices, bands):
            count = wide.shape[0]
            wide = jnp.concatenate(split(wide), axis=0)
            total = None
            for matrix, ones in zip(matrices, bands):
                if ones.shape[1] < matrix.shape[1]:
                    ones = jnp.concatenate([ones, ones], axis=1)
                seen = dot(wide, matrix)
                seen = (seen[:count] + seen[count:]) * ones
                more = dot_t(jnp.concatenate(split(seen), axis=0), matrix)
                total = more if total is None else total + more
            return total[:count] + total[count:]

        def sweep(step, vector):
            real, imag = vector
            real, imag = real * factor, imag * factor
            upper = jnp.concatenate([real, imag], axis=1)
            lower = jnp.concatenate([imag, -real], axis=1)
            stack = lambda low, high: jnp.concatenate([upper[low:high], lower[low:high]], axis=0)
            first = back_and_forth(stack(0, NEAR), pairs(mains, 0), [near[...]] * 4)
            second = back_and_forth(stack(WIN - FAR, WIN), pairs(mains, 128), [far[...]] * 4)
            third = back_and_forth(
                stack(WIN - LAST, WIN),
                [pixels(block) for block, _ in tails],
                [jnp.concatenate([ones, ones], axis=0) for _, ones in tails],
            )
            upper = merge(first[:NEAR], second[:FAR], third[:LAST])
            lower = merge(first[NEAR:], second[FAR:], third[LAST:])
            scale = factor * (1.0 / NBOX)
            real = (upper[:, :128] - lower[:, 128:]) * scale
            imag = (upper[:, 128:] + lower[:, :128]) * scale
            size = jnp.sum(real * real + imag * imag, axis=1, keepdims=True) / 128 + EPS
            norm = lax.rsqrt(size)
            return real * norm, imag * norm

        start = (jnp.ones((WIN, 128), jnp.float32), jnp.zeros((WIN, 128), jnp.float32))
        real, imag = lax.fori_loop(0, 4, sweep, start, unroll=True)
        linked[0, out_col * WIN : out_col * WIN + WIN] = real
        linked[1, out_col * WIN : out_col * WIN + WIN] = imag

    def send_back(tile):
        for part in range(2):
            value = linked[part, tile * 128 : tile * 128 + 128].T
            back[tile, part] = jnp.exp(value * CODE).astype(jnp.bfloat16)
        for peer in PEERS:
            back_copy(tile, peer).start()
        back_local(tile).start()

    place = lax.broadcasted_iota(jnp.int32, (LD, 128), 1)

    def assemble(out_col, part, tile):
        value = None
        done = 0
        while done < 128:
            k, window = (tile * 128 + done) // WIN, (tile * 128 + done) % WIN
            source, lane = (out_col * WIN + window) // 128, (out_col * WIN + window) % 128
            more = jnp.log(home[k, source, part].astype(jnp.float32)) * (1.0 / CODE)
            if lane != done:
                more = pltpu.roll(more, (done - lane) % 128, 1)
            value = more if value is None else jnp.where(place < done, value, more)
            done += min(WIN - window, 128 - lane, 128 - done)
        out_ref[part, :, out_col, tile * 128 : tile * 128 + 128] = value

    for out_col in range(4):
        if out_col == 0:
            for peer in range(1, NDATE + 1):
                side_copy(peer).wait_recv()

            @pl.when(strip == 0)
            def _():
                recv[0:4] = jnp.zeros((4, 2, 128, WIDE), jnp.bfloat16)

        for peer in PEERS:
            own_copy(out_col, peer).wait_recv()
        own_local(out_col).wait()
        link(out_col)
        if out_col:
            send_back(out_col - 1)

    for source in range(3):
        for peer in PEERS:
            back_copy(source, peer).wait_recv()
        back_local(source).wait()
        for out_col in ((0,), (1,), (2, 3))[source]:
            for part in range(2):
                for tile in range(6):
                    assemble(out_col, part, tile)

    for peer in PEERS:
        for chunk in range(4):
            own_copy(chunk, peer).wait_send()
        for tile in range(3):
            back_copy(tile, peer).wait_send()
    for peer in range(1, NDATE + 1):
        side_copy(peer).wait_send()


def on_device(acquisitions, valid_dates):
    dma = pltpu.SemaphoreType.DMA
    return pl.pallas_call(
        kernel,
        name="link_phases",
        out_shape=jax.ShapeDtypeStruct((2, LD, 4, 768), jnp.float32),
        in_specs=[pl.BlockSpec(memory_space=pl.ANY)] * 2,
        out_specs=pl.BlockSpec(memory_space=pltpu.VMEM),
        scratch_shapes=[
            pltpu.VMEM((2, LD, LC, ROWS), jnp.bfloat16),
            pltpu.VMEM((LD, LC, ROWS), jnp.int32),
            pltpu.VMEM((TILES, 2 * LD * LC, 128), jnp.float32),
            pltpu.VMEM((NDATE, BLOCKS, 2, LD, WIDE), jnp.bfloat16),
            pltpu.VMEM((BLOCKS, 2, 128, WIDE), jnp.bfloat16),
            pltpu.VMEM((2, 2 * 128, WIDE), jnp.bfloat16),
            pltpu.VMEM((2 * NEAR, 128), jnp.float32),
            pltpu.VMEM((2 * FAR, 128), jnp.float32),
            pltpu.VMEM((2, 4 * WIN, 128), jnp.float32),
            pltpu.VMEM((3, 2, 128, 128), jnp.bfloat16),
            pltpu.VMEM((NDATE, 3, 2, LD, 128), jnp.bfloat16),
            dma((2, 3)),
            dma((4, NDATE)),
            dma((4, NDATE)),
            dma((NDATE,)),
            dma((NDATE,)),
            dma((4,)),
            dma((3, NDATE)),
            dma((3, NDATE)),
            dma((3,)),
        ],
        compiler_params=pltpu.CompilerParams(
            collective_id=0, has_side_effects=True, vmem_limit_bytes=56 << 20
        ),
    )(acquisitions, valid_dates)


def solution(mesh):
    in_specs = (P(None, "date", "space", None), P("date", "space", None))
    out_specs = P(None, "date", "space", None)
    return jax.shard_map(
        on_device, mesh=mesh, in_specs=in_specs, out_specs=out_specs, check_vma=False
    )
```

```python
import jax
import jax.numpy as jnp
from jax import lax
from jax.experimental import pallas as pl
from jax.experimental.pallas import tpu as pltpu
from jax.sharding import PartitionSpec as P

MESH = pl.DeviceIdType.MESH
EPS = 1e-05
NBOX = 105
NDATE = 8
NSPACE = 16
LD = 16
LC = 24
ROWS = 2304
WIN = 96
WIDE = 256
NEAR = 48
FAR = 64
LAST = 16
TAIL = 44
TILES = ROWS // 128 + 2

CHUNKS = (
    (4, 9, (0, 4), 8, 0),
    (9, 16, (4, 10), 15, 1),
    (16, 23, (10, 16), 22, 2),
    (23, 30, (16, 22), 29, 3),
)
BLOCKS = 30
CODE = 7.5
USED = 22
ORDER = 7917224
PEERS = range(1, NDATE)


def block_of(col):
    if col < 0:
        return col + 3
    for first, _, (low, high), _, _ in CHUNKS:
        if low <= col < high:
            return first + col - low


def tails_of(out_col):
    low, high = 6 * out_col - 3, 6 * out_col + 3
    found = []
    if low < 0:
        found.append((3, 0, low + 3, 2))
    low = max(low, 0)
    for _, _, _, block, place in CHUNKS:
        if TAIL * low < WIDE * (place + 1) and TAIL * (high + 1) > WIDE * place:
            found.append((block, WIDE * place, low, high))
    return found


def dot(left, right):
    return lax.dot_general(
        left, right, (((1,), (0,)), ((), ())), preferred_element_type=jnp.float32
    )


def dot_t(left, right):
    return lax.dot_general(
        left, right, (((1,), (1,)), ((), ())), preferred_element_type=jnp.float32
    )


def split(value):
    high = value.astype(jnp.bfloat16)
    low = (value - high.astype(jnp.float32)).astype(jnp.bfloat16)
    return high, low


def kernel(
    acq_hbm, val_hbm, out_ref,
    acq, val, masked, send, recv, squares, near, far, linked, back, home,
    in_sem, send_sem, recv_sem, side_send, side_recv, own_sem,
    back_send, back_recv, back_own,
):
    me = lax.axis_index("date")
    strip = lax.axis_index("space")
    right = lax.rem(strip + 1, NSPACE)
    left = lax.rem(strip + NSPACE - 1, NSPACE)
    my_rows = pl.ds(pl.multiple_of(me * LD, LD), LD)

    def load(octet):
        cols = pl.ds(8 * octet, 8)
        return (
            pltpu.make_async_copy(
                acq_hbm.at[:, :, cols, :], acq.at[:, :, cols, :], in_sem.at[0, octet]
            ),
            pltpu.make_async_copy(
                val_hbm.at[:, cols, :], val.at[:, cols, :], in_sem.at[1, octet]
            ),
        )

    for copy in load(2):
        copy.start()

    barrier = pltpu.get_barrier_semaphore()
    for hop in range(1, NDATE):
        pl.semaphore_signal(
            barrier, inc=1, device_id=(lax.rem(me + hop, NDATE), strip), device_id_type=MESH
        )
    for hop in range(NDATE):
        pl.semaphore_signal(
            barrier, inc=1, device_id=(lax.rem(me + hop, NDATE), left), device_id_type=MESH
        )

    def inside(windows, first, rows):
        shape = (2 * windows, 128)
        row = lax.broadcasted_iota(jnp.int32, shape, 0)
        row = jnp.where(row >= windows, row - windows, row) + first
        at = lax.broadcasted_iota(jnp.int32, shape, 1) + rows
        return jnp.where((at >= 3 * row) & (at <= 3 * row + 14), 1.0, 0.0)

    near[...] = inside(NEAR, 0, 0)
    far[...] = inside(FAR, WIN - FAR, 128)

    masked[0] = jnp.zeros((2 * LD * LC, 128), jnp.float32)
    masked[TILES - 1] = jnp.zeros((2 * LD * LC, 128), jnp.float32)

    def mask(octet):
        if octet < 2:
            for copy in load(octet):
                copy.wait()

        def body(date, carry):
            cols = pl.ds(8 * octet, 8)
            valid = val[date, cols, :].astype(jnp.float32)
            for part in range(2):
                value = acq[part, date, cols, :].astype(jnp.float32) * valid
                at = pl.multiple_of(part * (LD * LC) + date * LC + 8 * octet, 8)
                for tile in range(TILES - 2):
                    masked[1 + tile, pl.ds(at, 8), :] = value[:, tile * 128 : tile * 128 + 128]
            return carry

        lax.fori_loop(0, LD, body, 0)

    def hop_of(turn):
        hop = (ORDER >> (3 * turn)) & 7
        mirrored = lax.rem(NDATE - hop // 2 * 2, NDATE) + lax.rem(hop, 2)
        return jnp.where(lax.rem(me // 2, 2) == 1, mirrored, hop)

    def peer_of(turn):
        hop = hop_of(turn)
        z = lax.rem(me, 2)
        return 2 * lax.rem(me // 2 + hop // 2, NDATE // 2) + lax.rem(z + hop, 2)

    def mask_for(octet, k):
        first = (122 + 288 * k) // 128

        def body(date, carry):
            cols = pl.ds(8 * octet, 8)
            for j in range(4):
                tile = jnp.clip(first + j, 1, TILES - 2)
                rows = pl.ds(pl.multiple_of((tile - 1) * 128, 128), 128)
                valid = val[date, cols, rows].astype(jnp.float32)
                for part in range(2):
                    value = acq[part, date, cols, rows].astype(jnp.float32) * valid
                    at = pl.multiple_of(part * (LD * LC) + date * LC + 8 * octet, 8)
                    masked[tile, pl.ds(at, 8), :] = value
            return carry

        lax.fori_loop(0, LD, body, 0, unroll=4)

    spot = lax.broadcasted_iota(jnp.int32, (LD, 128), 1)

    def turned(part, col, k, skip, count):
        first = 122 + 288 * k
        tile = first // 128
        rest = 128 - (first - tile * 128)
        at = pl.ds(part * (LD * LC) + col, LD, stride=LC)
        raw = [pltpu.roll(masked[tile + skip + j, at, :], rest, 1) for j in range(count + 1)]
        return [jnp.where(spot < rest, raw[j], raw[j + 1]) for j in range(count)]

    def pack_main(k, low, high, start):
        for col in range(low, high):
            for part in range(2):
                value = jnp.concatenate(turned(part, col, k, 0, 2), axis=1)
                send[k, start + col - low, part] = value.astype(jnp.bfloat16)

    def pack_tail(k, block, first, cols):
        for part in range(2):
            halves = [jnp.zeros((LD, 128), jnp.float32)] * 2
            for q, col in enumerate(cols):
                value = turned(part, col, k, 2, 1)[0]
                for half in range(2):
                    start = TAIL * q - first - 128 * half
                    if -TAIL < start < 128:
                        moved = pltpu.roll(value, start % 128, 1) if start % 128 else value
                        here = (spot >= start) & (spot < start + TAIL)
                        halves[half] = jnp.where(here, moved, halves[half])
            send[k, block, part] = jnp.concatenate(halves, axis=1).astype(jnp.bfloat16)

    def pack_tails(k, block, place):
        low, high = WIDE * place // TAIL, min((WIDE * place + WIDE - 1) // TAIL, USED - 1)
        pack_tail(k, block, WIDE * place - TAIL * low, range(low, high + 1))

    def own_copy(chunk, peer):
        low, high = CHUNKS[chunk][:2]
        to = peer_of(peer)
        hop = hop_of(peer)
        return pltpu.make_async_remote_copy(
            src_ref=send.at[to, low:high],
            dst_ref=recv.at[low:high, :, my_rows],
            send_sem=send_sem.at[chunk, hop],
            recv_sem=recv_sem.at[chunk, hop],
            device_id=(to, strip),
            device_id_type=MESH,
        )

    def own_local(chunk):
        low, high = CHUNKS[chunk][:2]
        return pltpu.make_async_copy(
            send.at[me, low:high], recv.at[low:high, :, my_rows], own_sem.at[chunk]
        )

    def side_copy(peer):
        to = peer_of(peer)
        hop = hop_of(peer)
        return pltpu.make_async_remote_copy(
            src_ref=send.at[to, 0:4],
            dst_ref=recv.at[0:4, :, my_rows],
            send_sem=side_send.at[hop],
            recv_sem=side_recv.at[hop],
            device_id=(to, right),
            device_id_type=MESH,
        )

    def back_copy(tile, peer):
        to = peer_of(peer)
        hop = hop_of(peer)
        rows = pl.ds(pl.multiple_of(to * LD, LD), LD)
        return pltpu.make_async_remote_copy(
            src_ref=back.at[tile, :, rows],
            dst_ref=home.at[me, tile],
            send_sem=back_send.at[tile, hop],
            recv_sem=back_recv.at[tile, hop],
            device_id=(to, strip),
            device_id_type=MESH,
        )

    def back_local(tile):
        return pltpu.make_async_copy(
            back.at[tile, :, my_rows], home.at[me, tile], back_own.at[tile]
        )

    for copy in load(2):
        copy.wait()
    for octet in range(2):
        for copy in load(octet):
            copy.start()

    def fill_side(turn):
        to = peer_of(turn)
        pack_main(to, 21, 24, 0)
        pack_tail(to, 3, 0, (21, 22, 23))

    def send_side(turn, carry):
        fill_side(turn)
        side_copy(turn).start()
        return carry

    mask_for(2, peer_of(1))
    fill_side(1)
    pl.semaphore_wait(barrier, 2 * NDATE - 1)
    side_copy(1).start()
    mask(2)
    lax.fori_loop(2, NDATE + 1, send_side, 0)
    mask(0)
    for chunk, (start, _, (low, high), block, place) in enumerate(CHUNKS):
        if chunk == 1:
            mask(1)

        def send_own(turn, carry):
            to = peer_of(turn)
            pack_main(to, low, high, start)
            pack_tails(to, block, place)

            @pl.when(turn < NDATE)
            def _():
                own_copy(chunk, turn).start()

            return carry

        lax.fori_loop(1, NDATE + 1, send_own, 0)
        own_local(chunk).start()

    def pixels(block):
        return recv[block].reshape(2 * 128, WIDE)

    def pairs(blocks, lanes):
        one = [recv[block, :, :, lanes : lanes + 128].reshape(2 * 128, 128) for block in blocks]
        return [
            jnp.concatenate(one[j : j + 2], axis=1) if j + 1 < len(one) else one[j]
            for j in range(0, len(one), 2)
        ]

    def tail_band(first, low, high):
        row = lax.broadcasted_iota(jnp.int32, (LAST, WIDE), 0) + (WIN - LAST)
        lane = lax.broadcasted_iota(jnp.int32, (LAST, WIDE), 1) + first
        at = lane - TAIL * low
        for q in range(low + 1, high + 1):
            at = jnp.where(lane >= TAIL * q, lane - TAIL * q, at)
        at = at + WIDE
        here = (lane >= TAIL * low) & (lane < TAIL * (high + 1))
        return jnp.where(here & (at >= 3 * row) & (at <= 3 * row + 14), 1.0, 0.0)

    def merge(first, second, third):
        both = first[WIN - FAR :] + second[: NEAR + FAR - WIN]
        middle = second[NEAR + FAR - WIN : FAR - LAST]
        end = second[FAR - LAST :] + third
        return jnp.concatenate([first[: WIN - FAR], both, middle, end], axis=0)

    def link(out_col):
        mains = [block_of(col) for col in range(6 * out_col - 3, 6 * out_col + 4)]
        tails = [
            (block, tail_band(first, low, high))
            for block, first, low, high in tails_of(out_col)
        ]

        for at in range(0, 2 * 128, 32):
            part, date = at // 128, at % 128
            total = jnp.zeros((32, WIDE), jnp.float32)
            for block in mains:
                value = recv[block, part, date : date + 32, :].astype(jnp.float32)
                total = total + value * value
            high, low = split(total)
            squares[0, at : at + 32, :] = high
            squares[1, at : at + 32, :] = low

        def power(ones, lanes):
            lanes = slice(lanes, lanes + 128)
            return dot_t(ones, squares[0, :, lanes]) + dot_t(ones, squares[1, :, lanes])

        last = jnp.zeros((LAST, 2 * 128), jnp.float32)
        for block, ones in tails:
            value = pixels(block).astype(jnp.float32)
            high, low = split(value * value)
            ones = ones.astype(jnp.bfloat16)
            last = last + dot_t(ones, high) + dot_t(ones, low)
        energy = merge(
            power(near[:NEAR].astype(jnp.bfloat16), 0),
            power(far[:FAR].astype(jnp.bfloat16), 128),
            last,
        )
        energy = (energy[:, :128] + energy[:, 128:]) / NBOX + EPS
        factor = lax.rsqrt(energy)

        def back_and_forth(wide, matrices, bands):
            count = wide.shape[0]
            wide = jnp.concatenate(split(wide), axis=0)
            total = None
            for matrix, ones in zip(matrices, bands):
                if ones.shape[1] < matrix.shape[1]:
                    ones = jnp.concatenate([ones, ones], axis=1)
                seen = dot(wide, matrix)
                seen = (seen[:count] + seen[count:]) * ones
                more = dot_t(jnp.concatenate(split(seen), axis=0), matrix)
                total = more if total is None else total + more
            return total[:count] + total[count:]

        def sweep(step, vector):
            real, imag = vector
            real, imag = real * factor, imag * factor
            upper = jnp.concatenate([real, imag], axis=1)
            lower = jnp.concatenate([imag, -real], axis=1)
            stack = lambda low, high: jnp.concatenate([upper[low:high], lower[low:high]], axis=0)
            first = back_and_forth(stack(0, NEAR), pairs(mains, 0), [near[...]] * 4)
            second = back_and_forth(stack(WIN - FAR, WIN), pairs(mains, 128), [far[...]] * 4)
            third = back_and_forth(
                stack(WIN - LAST, WIN),
                [pixels(block) for block, _ in tails],
                [jnp.concatenate([ones, ones], axis=0) for _, ones in tails],
            )
            upper = merge(first[:NEAR], second[:FAR], third[:LAST])
            lower = merge(first[NEAR:], second[FAR:], third[LAST:])
            scale = factor * (1.0 / NBOX)
            real = (upper[:, :128] - lower[:, 128:]) * scale
            imag = (upper[:, 128:] + lower[:, :128]) * scale
            size = jnp.sum(real * real + imag * imag, axis=1, keepdims=True) / 128 + EPS
            norm = lax.rsqrt(size)
            return real * norm, imag * norm

        start = (jnp.ones((WIN, 128), jnp.float32), jnp.zeros((WIN, 128), jnp.float32))
        real, imag = lax.fori_loop(0, 4, sweep, start, unroll=True)
        linked[0, out_col * WIN : out_col * WIN + WIN] = real
        linked[1, out_col * WIN : out_col * WIN + WIN] = imag

    def send_back(tile):
        for part in range(2):
            value = linked[part, tile * 128 : tile * 128 + 128].T
            back[tile, part] = jnp.exp(value * CODE).astype(jnp.bfloat16)
        for peer in PEERS:
            back_copy(tile, peer).start()
        back_local(tile).start()

    place = lax.broadcasted_iota(jnp.int32, (LD, 128), 1)

    def assemble(out_col, part, tile):
        value = None
        done = 0
        while done < 128:
            k, window = (tile * 128 + done) // WIN, (tile * 128 + done) % WIN
            source, lane = (out_col * WIN + window) // 128, (out_col * WIN + window) % 128
            more = jnp.log(home[k, source, part].astype(jnp.float32)) * (1.0 / CODE)
            if lane != done:
                more = pltpu.roll(more, (done - lane) % 128, 1)
            value = more if value is None else jnp.where(place < done, value, more)
            done += min(WIN - window, 128 - lane, 128 - done)
        out_ref[part, :, out_col, tile * 128 : tile * 128 + 128] = value

    for out_col in range(4):
        if out_col == 0:
            for peer in range(1, NDATE + 1):
                side_copy(peer).wait_recv()

            @pl.when(strip == 0)
            def _():
                recv[0:4] = jnp.zeros((4, 2, 128, WIDE), jnp.bfloat16)

        for peer in PEERS:
            own_copy(out_col, peer).wait_recv()
        own_local(out_col).wait()
        link(out_col)
        if out_col:
            send_back(out_col - 1)

    for source in range(3):
        for peer in PEERS:
            back_copy(source, peer).wait_recv()
        back_local(source).wait()
        for out_col in ((0,), (1,), (2, 3))[source]:
            for part in range(2):
                for tile in range(6):
                    assemble(out_col, part, tile)

    for peer in PEERS:
        for chunk in range(4):
            own_copy(chunk, peer).wait_send()
        for tile in range(3):
            back_copy(tile, peer).wait_send()
    for peer in range(1, NDATE + 1):
        side_copy(peer).wait_send()


def on_device(acquisitions, valid_dates):
    dma = pltpu.SemaphoreType.DMA
    return pl.pallas_call(
        kernel,
        name="link_phases",
        out_shape=jax.ShapeDtypeStruct((2, LD, 4, 768), jnp.float32),
        in_specs=[pl.BlockSpec(memory_space=pl.ANY)] * 2,
        out_specs=pl.BlockSpec(memory_space=pltpu.VMEM),
        scratch_shapes=[
            pltpu.VMEM((2, LD, LC, ROWS), jnp.bfloat16),
            pltpu.VMEM((LD, LC, ROWS), jnp.int32),
            pltpu.VMEM((TILES, 2 * LD * LC, 128), jnp.float32),
            pltpu.VMEM((NDATE, BLOCKS, 2, LD, WIDE), jnp.bfloat16),
            pltpu.VMEM((BLOCKS, 2, 128, WIDE), jnp.bfloat16),
            pltpu.VMEM((2, 2 * 128, WIDE), jnp.bfloat16),
            pltpu.VMEM((2 * NEAR, 128), jnp.float32),
            pltpu.VMEM((2 * FAR, 128), jnp.float32),
            pltpu.VMEM((2, 4 * WIN, 128), jnp.float32),
            pltpu.VMEM((3, 2, 128, 128), jnp.bfloat16),
            pltpu.VMEM((NDATE, 3, 2, LD, 128), jnp.bfloat16),
            dma((2, 3)),
            dma((4, NDATE)),
            dma((4, NDATE)),
            dma((NDATE,)),
            dma((NDATE,)),
            dma((4,)),
            dma((3, NDATE)),
            dma((3, NDATE)),
            dma((3,)),
        ],
        compiler_params=pltpu.CompilerParams(
            collective_id=0, has_side_effects=True, vmem_limit_bytes=56 << 20
        ),
    )(acquisitions, valid_dates)


def solution(mesh):
    in_specs = (P(None, "date", "space", None), P("date", "space", None))
    out_specs = P(None, "date", "space", None)
    return jax.shard_map(
        on_device, mesh=mesh, in_specs=in_specs, out_specs=out_specs, check_vma=False
    )
```
